128 devices in a mesh: dp: 8 (over y, x_lo), tensor: 16 (over x_hi, z, core).
Axes of the slice: x: 4 (x_hi: 2, x_lo: 2; x = x_hi * 2 + x_lo), y: 4, z: 4, core: 2. Of those that a mesh axis runs over, the one named last changes fastest.
Arguments:
- tokens: bfloat16 [8192, 8192], P('dp', 'tensor'), may hold values from -6 to 6
- packing: int32 [8, 6], replicated, may hold values from 0 to 63, as said below
- tail_tokens: int32 [8], replicated, may hold values from 1 to 128
- mix_ratio: int32 [2], replicated, may hold values from 1 to 32, as said below
- policy_gate: bfloat16 [8192, 14336], P(('dp', 'tensor')), may hold values from -6 to 6
- policy_up: bfloat16 [8192, 14336], P(('dp', 'tensor')), may hold values from -6 to 6
- reference_gate: bfloat16 [8192, 14336], P('dp', 'tensor'), may hold values from -6 to 6
- reference_up: bfloat16 [8192, 14336], P('dp', 'tensor'), may hold values from -6 to 6
Outputs:
- new_gate: bfloat16 [8192, 14336], P('dp', 'tensor')
- new_up: bfloat16 [8192, 14336], P('dp', 'tensor')
- hidden: bfloat16 [6144, 14336], P('dp', 'tensor')
The draws below stay inside these ranges and needn't reach their ends.
Inputs may be any that keep to these rules, and one draw needn't show every extreme that they name: `packing`: each entry is g * 8 + b for a data group g and block b; the blocks named for group g are exactly its blocks 0 to count - 1, each once; a reference group takes at most one block from any data group; one data group has all 8 of its blocks named. mix_ratio[1] is 32 and mix_ratio[0] lies between 1 and 31.
All inputs are finite; a program needn't handle non-finite values.
Results may differ from the reference program's by a relative error of at most 0.02.
Values may be sent and summed in bfloat16 or wider, within the bound.
No kernel may reach another device: no remote copies, remote signals or barrier semaphores. Data moves between devices by JAX's collectives and lax.ppermute only.
A program may use at most 128 MiB of HBM per device.

```python
import math
import jax
import jax.numpy as jnp
from jax import lax

D = 8192
FFW = 14336
BLOCK = 128
GB = 6
SB = 8
N_DP = 8


def draw_packing(key, part):
    first_key = jax.random.fold_in(key, 11)
    second_key = jax.random.fold_in(key, 12)
    third_key = jax.random.fold_in(key, 13)
    order = jax.random.permutation(first_key, N_DP).astype(jnp.int32)
    others = order[1:]
    offset = jax.random.randint(second_key, (), 0, N_DP - 1)
    dest_ids = jnp.arange(N_DP, dtype=jnp.int32)[:, None]
    slot_ids = jnp.arange(GB, dtype=jnp.int32)[None, :]
    spread_index = (dest_ids * (GB - 1) + slot_ids - 1 + offset) % (N_DP - 1)
    sources = jnp.where(slot_ids == 0, order[0], others[spread_index])
    flat_sources = sources.reshape(-1)
    one_hot = (flat_sources[:, None] == jnp.arange(N_DP, dtype=jnp.int32)[None, :]).astype(jnp.int32)
    earlier = jnp.cumsum(one_hot, axis=0) - one_hot
    block_ids = jnp.sum(earlier * one_hot, axis=1)
    entries = (flat_sources * SB + block_ids).reshape(N_DP, GB)
    row_keys = jax.random.split(third_key, N_DP)
    shuffles = jax.vmap(lambda row_key: jax.random.permutation(row_key, GB))(row_keys)
    return jnp.take_along_axis(entries, shuffles, axis=1).astype(jnp.int32)


def draw_mix_ratio(key, part):
    numer_key = jax.random.fold_in(key, 22)
    denominator = jnp.full((), 32, jnp.int32)
    numerator = jax.random.randint(numer_key, (), 1, 32)
    return jnp.stack([numerator, denominator]).astype(jnp.int32)


def touch_ends(array, own_key, low, high):
    shape = array.shape
    place = [jax.random.randint(jax.random.fold_in(own_key, axis), (), 0, shape[axis]) for axis in range(len(shape))]
    array = array.at[tuple(place)].set(low)
    longest = shape.index(max(shape))
    place[longest] = (place[longest] + 1) % shape[longest]
    return array.at[tuple(place)].set(high)


def level_of(rng, dims, cuts, least, largest):
    factor_of, own = 1.0, jax.random.fold_in(rng, 6)
    for position, blocks in cuts:
        heights = jnp.exp(jax.random.uniform(jax.random.fold_in(own, position), (blocks,), jnp.float32, least / len(cuts), largest / len(cuts)))
        factor_of = factor_of * jnp.repeat(heights, dims[position] // blocks).reshape([-1 if axis == position else 1 for axis in range(len(dims))])
    return factor_of


def scatter_about(key, extent, deviation, limit, cuts=(), held_as=jnp.bfloat16):
    values = jax.random.normal(key, extent, jnp.float32) * deviation
    if len(cuts) > 0:
        values = level_of(key, extent, cuts, -0.22, 0.18) * values
    return jnp.clip(values, min=-limit, max=limit).astype(held_as)


def setup_inputs(seed: int = 0) -> dict:
    splits = jax.random.split(jax.random.key(seed), 9)
    return {
        "tokens": scatter_about(splits[0], (N_DP * SB * BLOCK, D), 1.0, 6.0, ((0, 8), (1, 16))),
        "packing": draw_packing(jax.random.fold_in(splits[8], 71), 0),
        "tail_tokens": touch_ends(jax.random.randint(splits[2], (N_DP,), 1, BLOCK + 1), jax.random.fold_in(splits[2], 1), 1, BLOCK).astype(jnp.int32),
        "mix_ratio": draw_mix_ratio(jax.random.fold_in(splits[8], 71), 0),
        "policy_gate": scatter_about(splits[4], (D, FFW), 1.0, 6.0, ((0, 128),)),
        "policy_up": scatter_about(splits[5], (D, FFW), 1.0, 6.0, ((0, 128),)),
        "reference_gate": scatter_about(splits[6], (D, FFW), 1.0, 6.0, ((0, 8), (1, 16))),
        "reference_up": scatter_about(splits[7], (D, FFW), 1.0, 6.0, ((0, 8), (1, 16))),
    }


def blend_into(policy_part, old_part, weight_ratio):
    mixed = weight_ratio * policy_part.astype(jnp.float32) + (1.0 - weight_ratio) * old_part.astype(jnp.float32)
    return mixed.astype(jnp.bfloat16)

def reference(tokens, packing, tail_tokens, mix_ratio, policy_gate, policy_up, reference_gate, reference_up):
    weight_ratio = mix_ratio[0].astype(jnp.float32) / mix_ratio[1].astype(jnp.float32)
    new_gate = blend_into(policy_gate, reference_gate, weight_ratio)
    new_up = blend_into(policy_up, reference_up, weight_ratio)
    source = packing // SB
    group_ids = jnp.arange(N_DP, dtype=jnp.int32)
    counts = lax.optimization_barrier(jnp.sum((source.reshape(-1)[:, None] == group_ids[None, :]).astype(jnp.int32), axis=0))
    row_limit = (counts - 1) * BLOCK + tail_tokens
    grouped = tokens.reshape(N_DP, SB * BLOCK, D)
    keep_mask = jnp.arange(SB * BLOCK, dtype=jnp.int32)[None, :] < row_limit[:, None]
    masked_rows = jnp.where(keep_mask[:, :, None], grouped, jnp.zeros((), jnp.bfloat16))
    blocks = masked_rows.reshape(N_DP * SB, BLOCK, D)
    packed = jnp.take(blocks, packing.reshape(-1).astype(jnp.int32), axis=0).reshape(N_DP * GB * BLOCK, D)
    row_width = D // N_DP
    row_total = N_DP * GB * BLOCK
    packed_blocks = packed.reshape(row_total, N_DP, row_width).transpose(1, 0, 2)
    gate_blocks = new_gate.reshape(N_DP, row_width, FFW)
    up_blocks = new_up.reshape(N_DP, row_width, FFW)

    def add_block(carry, items):
        columns, gate_rows, up_rows = items
        gate_part = jnp.dot(columns, gate_rows, preferred_element_type=jnp.float32).astype(jnp.bfloat16)
        up_part = jnp.dot(columns, up_rows, preferred_element_type=jnp.float32).astype(jnp.bfloat16)
        return ((carry[0] + gate_part.astype(jnp.float32), carry[1] + up_part.astype(jnp.float32)), None)
    start = (jnp.zeros((row_total, FFW), jnp.float32), jnp.zeros((row_total, FFW), jnp.float32))
    totals, unused = lax.scan(add_block, start, (packed_blocks, gate_blocks, up_blocks))
    inv_width = 1.0 / math.sqrt(D)
    gate_sum = totals[0] * inv_width
    up_sum = totals[1] * inv_width
    hidden = (jax.nn.silu(gate_sum) * up_sum).astype(jnp.bfloat16)
    return (new_gate, new_up, hidden)
```

```python
import math

import jax
import jax.numpy as jnp
from jax import lax
from jax.experimental import pallas as pl
from jax.experimental.pallas import tpu as pltpu
from jax.sharding import Mesh
from jax.sharding import PartitionSpec as P


NY, NXL, NXH, NZ, NC = 4, 2, 2, 4, 2
SB = 8
AXES = ("y", "xl", "xh", "z", "core")
DP = ("y", "xl")
TENSOR = ("xh", "z", "core")


def lin(y, xl, xh, z, c):
    return (((y * NXL + xl) * NXH + xh) * NZ + z) * NC + c


def every():
    for y in range(NY):
        for xl in range(NXL):
            for xh in range(NXH):
                for z in range(NZ):
                    for c in range(NC):
                        yield y, xl, xh, z, c


def shift_perm(dy=0, dxl=0, dxh=0, dz=0, dc=0):
    return [
        (
            lin(y, xl, xh, z, c),
            lin(
                (y + dy) % NY,
                (xl + dxl) % NXL,
                (xh + dxh) % NXH,
                (z + dz) % NZ,
                (c + dc) % NC,
            ),
        )
        for y, xl, xh, z, c in every()
    ]


def send(x, perm):
    return lax.ppermute(x, AXES, perm)


def blend_into(policy_part, old_part, weight_ratio):
    mixed = weight_ratio * policy_part.astype(jnp.float32) + (1.0 - weight_ratio) * old_part.astype(
        jnp.float32
    )
    return mixed.astype(jnp.bfloat16)


def partial_sums(held, k, new, other):
    pieces = [(x, k[h]) for h in range(2) for x in held[h]]
    rows, full = pieces[0][0].shape[1:]
    width = new.shape[1]
    tall = rows * len(held[0])
    step = full // 2

    def kernel(*refs):
        x_refs = refs[: len(pieces)]
        new_ref, other_ref, out_0, out_1, acc = refs[len(pieces) :]
        i = pl.program_id(0)

        def product(w_ref):
            x = jnp.concatenate([r[0] for r in x_refs], axis=0)
            return jnp.dot(x, w_ref[...], preferred_element_type=jnp.float32)

        @pl.when(i == 0)
        def _():
            acc[...] = product(new_ref)

        @pl.when(i == 1)
        def _():
            total = acc[...] + product(other_ref)
            out_0[...] = total[:tall].astype(jnp.bfloat16)
            out_1[...] = total[tall:].astype(jnp.bfloat16)

    def x_spec(k):
        return pl.BlockSpec((1, rows, step), lambda i: (k, 0, i))

    out_spec = pl.BlockSpec((tall, width), lambda i: (0, 0))
    return pl.pallas_call(
        kernel,
        grid=(2,),
        in_specs=[x_spec(k) for _, k in pieces]
        + [
            pl.BlockSpec((step, width), lambda i: (0, 0)),
            pl.BlockSpec((step, width), lambda i: (0, 0)),
        ],
        out_specs=[out_spec, out_spec],
        out_shape=[jax.ShapeDtypeStruct((tall, width), jnp.bfloat16)] * 2,
        scratch_shapes=[pltpu.VMEM((2 * tall, width), jnp.float32)],
        cost_estimate=pl.CostEstimate(
            flops=4 * tall * full * width, bytes_accessed=10_000_000, transcendentals=0
        ),
    )(*[x for x, _ in pieces], new, other)


def body(
    tokens, packing, tail_tokens, mix_ratio, policy_gate, policy_up, reference_gate, reference_up
):
    weight_ratio = mix_ratio[0].astype(jnp.float32) / mix_ratio[1].astype(jnp.float32)
    groups, slots = packing.shape
    block = tokens.shape[0] // SB
    feat = tokens.shape[1]
    width = reference_gate.shape[1]
    my_y, my_xl = lax.axis_index("y"), lax.axis_index("xl")
    my_xh, my_z, my_c = lax.axis_index("xh"), lax.axis_index("z"), lax.axis_index("core")
    my_group = my_y * NXL + my_xl

    tens = NXH * NZ * NC
    sub = block // tens
    my_t = (my_xh * NZ + my_z) * NC + my_c
    source = packing // SB
    from_here = source == my_group
    count = jnp.sum(from_here.astype(jnp.int32))
    row_limit = (count - 1) * block + jnp.sum(
        jnp.where(jnp.arange(groups) == my_group, tail_tokens, 0)
    )
    chosen = jnp.sum(jnp.where(from_here, packing % SB, 0), axis=1)
    live = jnp.where(jnp.any(from_here, axis=1), row_limit - chosen * block, 0)

    lines = policy_gate.shape[0]

    def at(x, i, axis):
        return lax.dynamic_index_in_dim(x, i, axis, keepdims=False)

    def turn(policy, first):
        chunks = (
            policy.reshape(lines, tens, width)
            .transpose(1, 0, 2)
            .reshape(NXH, NZ, NC, lines, width)
        )
        came = send(at(chunks, my_xh ^ 1, 0), shift_perm(dxh=1))
        if first is not None:
            came, _ = lax.optimization_barrier((came, first))
        chunks = jnp.stack([at(chunks, my_xh, 0), came])
        chunks = jnp.stack(
            [
                at(chunks, my_c, 2),
                send(at(chunks, my_c ^ 1, 2), shift_perm(dc=1)),
            ]
        )
        given = [at(chunks, (my_z + dz) & 3, 2) for dz in range(1, NZ)]
        return given, [at(chunks, my_z, 2)] + [
            send(x, shift_perm(dz=dz)) for dz, x in enumerate(given, 1)
        ]

    news = []
    others = []

    def blend(turned, old):
        xh, z, c = (
            lax.broadcasted_iota(jnp.int32, (NXH, NZ, NC), i).reshape(-1) for i in range(3)
        )
        place = ((((my_z - z) & 3) * NC) + (c ^ my_c)) * NXH + (xh ^ my_xh)
        moved = jnp.take(jnp.stack(turned).reshape(tens, lines, width), place, axis=0)
        new = blend_into(moved.reshape(tens * lines, width), old, weight_ratio)
        news.append(new)
        others.append(send(new, shift_perm(dxl=1)))

    given, turned_gate = turn(policy_gate, None)
    given, turned_up = turn(policy_up, given)
    rows = lax.all_to_all(
        tokens.reshape(SB, tens, sub, feat).transpose(1, 0, 2, 3),
        TENSOR,
        split_axis=0,
        concat_axis=0,
        tiled=True,
    )
    a, xl, gy, b = (
        lax.broadcasted_iota(jnp.int32, (NY, NXL, NY, 4), i).reshape(-1) for i in range(4)
    )
    hot = (gy * NXL + xl)[:, None] == jnp.arange(groups)[None, :]
    block_of = jnp.sum(jnp.where(hot, chosen[None, :], 0), axis=1)
    live_of = jnp.sum(jnp.where(hot, live[None, :], 0), axis=1) - my_t * sub
    outgoing = jnp.take(rows.reshape(tens * SB, sub, feat), (a * 4 + b) * SB + block_of, axis=0)
    keep = jnp.arange(sub, dtype=jnp.int32)[None, :] < live_of[:, None]
    outgoing = jnp.where(keep[:, :, None], outgoing, jnp.zeros((), jnp.bfloat16))
    arrived = lax.all_to_all(
        outgoing.reshape(groups, NY * 4 * sub, feat), DP, split_axis=0, concat_axis=0, tiled=True
    )
    k, b, slot = (
        lax.broadcasted_iota(jnp.int32, (NY, 4, slots), i).reshape(-1) for i in range(3)
    )
    gy = (my_y + k) & 3
    hot = ((gy * NXL + my_xl) * slots + slot)[:, None] == jnp.arange(groups * slots)[None, :]
    from_of = jnp.sum(jnp.where(hot, source.reshape(-1)[None, :], 0), axis=1)
    packed = jnp.take(
        arrived.reshape(groups * NY * 4, sub, feat),
        (from_of * NY + gy) * 4 + (b ^ (2 * my_xl)),
        axis=0,
    )
    packed = (
        packed.reshape(NY, 4, slots * sub, feat)
        .transpose(0, 2, 1, 3)
        .reshape(NY, slots * sub, 4 * feat)
    )
    crossed = send(packed, shift_perm(dxh=1))
    turned_gate, _ = lax.optimization_barrier((turned_gate, packed))
    blend(turned_gate, reference_gate)
    turned_up, _ = lax.optimization_barrier((turned_up, (crossed, news[0])))
    blend(turned_up, reference_up)
    held = []
    for h, mine in enumerate((packed, crossed)):
        low = send(mine, shift_perm(dz=1))
        high = send(mine, shift_perm(dz=-1))
        if h == 0:
            far = send(low, shift_perm(dz=1))
        else:
            far = send(high, shift_perm(dz=-1))
        here = (mine, high, far, low)
        there = [send(x, shift_perm(dc=1)) for x in here]
        held.append([x for pair in zip(here, there) for x in pair])

    def way(p, h):
        return 1 if (h + p) % 2 == 0 else -1

    def parts_of(p, s):
        k = [(way(p, h) * (NY - 1 - s)) % NY for h in range(2)]
        return partial_sums(held, k, news[p], others[p])

    inv_width = 1.0 / math.sqrt(feat * tens)
    acc = {}
    sums = {}
    for s in range(NY):
        for p in range(2):
            parts = parts_of(p, s)
            for h in range(2):
                part = parts[h].astype(jnp.float32)
                if s > 0:
                    part = part + acc[p, h].astype(jnp.float32)
                if s < NY - 1:
                    acc[p, h] = send(part.astype(jnp.bfloat16), shift_perm(dy=way(p, h)))
                else:
                    sums[p, h] = part * inv_width
    hidden = [(jax.nn.silu(sums[0, h]) * sums[1, h]).astype(jnp.bfloat16) for h in range(2)]
    xh, z, c = (lax.broadcasted_iota(jnp.int32, (NXH, NZ, NC), i).reshape(-1) for i in range(3))
    place = (((xh ^ my_xh) * NZ) + ((z - my_z) & 3)) * NC + (c ^ my_c)
    hidden = jnp.concatenate(hidden, axis=0).reshape(tens, slots * sub, width)
    hidden = (
        jnp.take(hidden, place, axis=0)
        .reshape(tens, slots, sub, width)
        .transpose(1, 0, 2, 3)
        .reshape(slots * block, width)
    )
    return (news[0], news[1], hidden)


def solution(mesh):
    fine = Mesh(mesh.devices.reshape(NY, NXL, NXH, NZ, NC), AXES)
    in_specs = (
        P(DP, TENSOR),
        P(),
        P(),
        P(),
        P(AXES, None),
        P(AXES, None),
        P(DP, TENSOR),
        P(DP, TENSOR),
    )
    out_specs = (P(DP, TENSOR), P(DP, TENSOR), P(DP, TENSOR))

    return jax.shard_map(body, mesh=fine, in_specs=in_specs, out_specs=out_specs, check_vma=False)
```

```python
import math

import jax
import jax.numpy as jnp
from jax import lax
from jax.experimental import pallas as pl
from jax.experimental.pallas import tpu as pltpu
from jax.sharding import Mesh
from jax.sharding import PartitionSpec as P


NY, NXL, NXH, NZ, NC = 4, 2, 2, 4, 2
SB = 8
AXES = ("y", "xl", "xh", "z", "core")
DP = ("y", "xl")
TENSOR = ("xh", "z", "core")


def lin(y, xl, xh, z, c):
    return (((y * NXL + xl) * NXH + xh) * NZ + z) * NC + c


def every():
    for y in range(NY):
        for xl in range(NXL):
            for xh in range(NXH):
                for z in range(NZ):
                    for c in range(NC):
                        yield y, xl, xh, z, c


def shift_perm(dy=0, dxl=0, dxh=0, dz=0, dc=0):
    return [
        (
            lin(y, xl, xh, z, c),
            lin(
                (y + dy) % NY,
                (xl + dxl) % NXL,
                (xh + dxh) % NXH,
                (z + dz) % NZ,
                (c + dc) % NC,
            ),
        )
        for y, xl, xh, z, c in every()
    ]


def send(x, perm):
    return lax.ppermute(x, AXES, perm)


def blend_into(policy_part, old_part, weight_ratio):
    mixed = weight_ratio * policy_part.astype(jnp.float32) + (1.0 - weight_ratio) * old_part.astype(
        jnp.float32
    )
    return mixed.astype(jnp.bfloat16)


def partial_sums(held, k, new, other):
    pieces = [(x, k[h]) for h in range(2) for x in held[h]]
    rows, full = pieces[0][0].shape[1:]
    width = new.shape[1]
    tall = rows * len(held[0])
    step = full // 2
    half = len(held[0])

    def kernel(*refs):
        x_refs = refs[: len(pieces)]
        new_ref, other_ref, out_0, out_1, acc, tile = refs[len(pieces) :]
        i = pl.program_id(0)

        @pl.loop(0, 4)
        def _(q):
            part = pl.ds(pl.multiple_of(q * (step // 4), step // 4), step // 4)
            for j, r in enumerate(x_refs):
                tile[j // half, pl.ds((j % half) * rows, rows), part] = r[0, :, part]

        def product(w_ref, h):
            return jnp.dot(tile[h], w_ref[...], preferred_element_type=jnp.float32)

        @pl.when(i == 0)
        def _():
            @pl.loop(0, 2)
            def _(h):
                acc[h] = product(new_ref, h)

        @pl.when(i == 1)
        def _():
            @pl.loop(0, 2)
            def _(h):
                acc[h] = acc[h] + product(other_ref, h)

            @pl.loop(0, half)
            def _(j):
                part = pl.ds(pl.multiple_of(j * rows, rows), rows)
                out_0[part] = acc[0, part].astype(jnp.bfloat16)
                out_1[part] = acc[1, part].astype(jnp.bfloat16)

    def x_spec(k):
        return pl.BlockSpec((1, rows, step), lambda i: (k, 0, i))

    return pl.pallas_call(
        kernel,
        grid=(2,),
        in_specs=[x_spec(k) for _, k in pieces]
        + [
            pl.BlockSpec((step, width), lambda i: (0, 0)),
            pl.BlockSpec((step, width), lambda i: (0, 0)),
        ],
        out_specs=[pl.BlockSpec((tall, width), lambda i: (0, 0))] * 2,
        out_shape=[jax.ShapeDtypeStruct((tall, width), jnp.bfloat16)] * 2,
        scratch_shapes=[
            pltpu.VMEM((2, tall, width), jnp.float32),
            pltpu.VMEM((2, tall, step), jnp.bfloat16),
        ],
        cost_estimate=pl.CostEstimate(
            flops=4 * tall * full * width, bytes_accessed=10_000_000, transcendentals=0
        ),
    )(*[x for x, _ in pieces], new, other)


def finish(parts, sums, place, slots, scale):
    tall, width = parts[0, 0].shape
    rows = tall // (NZ * NC)
    sub = rows // slots
    keys = [(p, h) for h in range(2) for p in range(2)]

    def kernel(place_ref, *refs):
        out = refs[-1]
        for h in range(2):

            @pl.loop(0, NC)
            def _(c, h=h):
                part = pl.ds(pl.multiple_of(c * rows, rows), rows)
                gate, up = (
                    (
                        refs[4 * h + 2 * p][part].astype(jnp.float32)
                        + refs[4 * h + 2 * p + 1][part].astype(jnp.float32)
                    )
                    * scale
                    for p in range(2)
                )
                hidden = (gate / (1.0 + jnp.exp(-gate)) * up).astype(jnp.bfloat16)
                out[:, pl.ds(place_ref[0] ^ h, 1), :, pl.ds(place_ref[2] ^ c, 1)] = hidden.reshape(
                    slots, 1, 1, 1, sub, width
                )

    spec = pl.BlockSpec((NC * rows, width), lambda i, place: (i, 0))
    return pl.pallas_call(
        kernel,
        grid_spec=pltpu.PrefetchScalarGridSpec(
            num_scalar_prefetch=1,
            grid=(NZ,),
            in_specs=[spec] * 8,
            out_specs=pl.BlockSpec(
                (slots, NXH, 1, NC, sub, width),
                lambda i, place: (0, 0, (place[1] + i) & 3, 0, 0, 0),
            ),
        ),
        out_shape=jax.ShapeDtypeStruct((slots, NXH, NZ, NC, sub, width), jnp.bfloat16),
    )(place, *[x for key in keys for x in (parts[key], sums[key])])


def body(
    tokens, packing, tail_tokens, mix_ratio, policy_gate, policy_up, reference_gate, reference_up
):
    weight_ratio = mix_ratio[0].astype(jnp.float32) / mix_ratio[1].astype(jnp.float32)
    groups, slots = packing.shape
    block = tokens.shape[0] // SB
    feat = tokens.shape[1]
    width = reference_gate.shape[1]
    my_y, my_xl = lax.axis_index("y"), lax.axis_index("xl")
    my_xh, my_z, my_c = lax.axis_index("xh"), lax.axis_index("z"), lax.axis_index("core")
    my_group = my_y * NXL + my_xl

    tens = NXH * NZ * NC
    sub = block // tens
    my_t = (my_xh * NZ + my_z) * NC + my_c
    source = packing // SB
    from_here = source == my_group
    count = jnp.sum(from_here.astype(jnp.int32))
    row_limit = (count - 1) * block + jnp.sum(
        jnp.where(jnp.arange(groups) == my_group, tail_tokens, 0)
    )
    chosen = jnp.sum(jnp.where(from_here, packing % SB, 0), axis=1)
    live = jnp.where(jnp.any(from_here, axis=1), row_limit - chosen * block, 0)

    lines = policy_gate.shape[0]

    def at(x, i, axis):
        return lax.dynamic_index_in_dim(x, i, axis, keepdims=False)

    def turn(policy, first):
        chunks = (
            policy.reshape(lines, tens, width)
            .transpose(1, 0, 2)
            .reshape(NXH, NZ, NC, lines, width)
        )
        came = send(at(chunks, my_xh ^ 1, 0), shift_perm(dxh=1))
        if first is not None:
            came, _ = lax.optimization_barrier((came, first))
        chunks = jnp.stack([at(chunks, my_xh, 0), came])
        chunks = jnp.stack(
            [
                at(chunks, my_c, 2),
                send(at(chunks, my_c ^ 1, 2), shift_perm(dc=1)),
            ]
        )
        given = [at(chunks, (my_z + dz) & 3, 2) for dz in range(1, NZ)]
        return given, [at(chunks, my_z, 2)] + [
            send(x, shift_perm(dz=dz)) for dz, x in enumerate(given, 1)
        ]

    news = []
    others = []

    def blend(turned, old):
        xh, z, c = (
            lax.broadcasted_iota(jnp.int32, (NXH, NZ, NC), i).reshape(-1) for i in range(3)
        )
        place = ((((my_z - z) & 3) * NC) + (c ^ my_c)) * NXH + (xh ^ my_xh)
        moved = jnp.take(jnp.stack(turned).reshape(tens, lines, width), place, axis=0)
        new = blend_into(moved.reshape(tens * lines, width), old, weight_ratio)
        news.append(new)
        others.append(send(new, shift_perm(dxl=1)))

    given, turned_gate = turn(policy_gate, None)
    given, turned_up = turn(policy_up, given)
    rows = lax.all_to_all(
        tokens.reshape(SB, tens, sub, feat).transpose(1, 0, 2, 3),
        TENSOR,
        split_axis=0,
        concat_axis=0,
        tiled=True,
    )
    a, xl, gy, b = (
        lax.broadcasted_iota(jnp.int32, (NY, NXL, NY, 4), i).reshape(-1) for i in range(4)
    )
    hot = (gy * NXL + xl)[:, None] == jnp.arange(groups)[None, :]
    block_of = jnp.sum(jnp.where(hot, chosen[None, :], 0), axis=1)
    live_of = jnp.sum(jnp.where(hot, live[None, :], 0), axis=1) - my_t * sub
    outgoing = jnp.take(rows.reshape(tens * SB, sub, feat), (a * 4 + b) * SB + block_of, axis=0)
    keep = jnp.arange(sub, dtype=jnp.int32)[None, :] < live_of[:, None]
    outgoing = jnp.where(keep[:, :, None], outgoing, jnp.zeros((), jnp.bfloat16))
    arrived = lax.all_to_all(
        outgoing.reshape(groups, NY * 4 * sub, feat), DP, split_axis=0, concat_axis=0, tiled=True
    )
    k, b, slot = (
        lax.broadcasted_iota(jnp.int32, (NY, 4, slots), i).reshape(-1) for i in range(3)
    )
    gy = (my_y + k) & 3
    hot = ((gy * NXL + my_xl) * slots + slot)[:, None] == jnp.arange(groups * slots)[None, :]
    from_of = jnp.sum(jnp.where(hot, source.reshape(-1)[None, :], 0), axis=1)
    packed = jnp.take(
        arrived.reshape(groups * NY * 4, sub, feat),
        (from_of * NY + gy) * 4 + (b ^ (2 * my_xl)),
        axis=0,
    )
    packed = (
        packed.reshape(NY, 4, slots * sub, feat)
        .transpose(0, 2, 1, 3)
        .reshape(NY, slots * sub, 4 * feat)
    )
    crossed = send(packed, shift_perm(dxh=1))
    turned_gate, _ = lax.optimization_barrier((turned_gate, packed))
    blend(turned_gate, reference_gate)
    turned_up, _ = lax.optimization_barrier((turned_up, (crossed, news[0])))
    blend(turned_up, reference_up)
    held = []
    for h, mine in enumerate((packed, crossed)):
        low = send(mine, shift_perm(dz=1))
        high = send(mine, shift_perm(dz=-1))
        if h == 0:
            far = send(low, shift_perm(dz=1))
        else:
            far = send(high, shift_perm(dz=-1))
        here = (mine, high, far, low)
        there = [send(x, shift_perm(dc=1)) for x in here]
        held.append([x for pair in zip(here, there) for x in pair])

    def way(p, h):
        return 1 if (h + p) % 2 == 0 else -1

    def parts_of(p, s):
        k = [(way(p, h) * (NY - 1 - s)) % NY for h in range(2)]
        return partial_sums(held, k, news[p], others[p])

    inv_width = 1.0 / math.sqrt(feat * tens)
    acc = {}
    last = {}
    for s in range(NY):
        for p in range(2):
            parts = parts_of(p, s)
            for h in range(2):
                if s == NY - 1:
                    last[p, h] = parts[h]
                    continue
                part = parts[h].astype(jnp.float32)
                if s > 0:
                    part = part + acc[p, h].astype(jnp.float32)
                acc[p, h] = send(part.astype(jnp.bfloat16), shift_perm(dy=way(p, h)))
    place = jnp.stack([my_xh, my_z, my_c]).astype(jnp.int32)
    hidden = finish(last, acc, place, slots, inv_width).reshape(slots * block, width)
    return (news[0], news[1], hidden)


def solution(mesh):
    fine = Mesh(mesh.devices.reshape(NY, NXL, NXH, NZ, NC), AXES)
    in_specs = (
        P(DP, TENSOR),
        P(),
        P(),
        P(),
        P(AXES, None),
        P(AXES, None),
        P(DP, TENSOR),
        P(DP, TENSOR),
    )
    out_specs = (P(DP, TENSOR), P(DP, TENSOR), P(DP, TENSOR))

    return jax.shard_map(body, mesh=fine, in_specs=in_specs, out_specs=out_specs, check_vma=False)
```
